32 devices in a mesh: section: 4 (over x, core), mp: 8 (over z, y).
Axes of the slice: x: 2, y: 2, z: 4, core: 2. Of those that a mesh axis runs over, the one named last changes fastest.
Arguments:
- activations: bfloat16 [4, 64, 4096], P('section', 'mp'), may hold values from -24 to 24
- enc_weight: bfloat16 [4, 4096, 4096], P('section', None, 'mp'), may hold values from -0.046875 to 0.046875
- enc_bias: float32 [4096], P('mp'), may hold values from -4 to 4
- dec_weight: bfloat16 [4096, 4, 4096], P('mp', 'section'), may hold values from -2.1875 to 2.1875
- dec_bias: float32 [4, 4096], P('section'), may hold values from -3 to 3
Outputs:
- loss: float32 [], replicated
- grad_dec: bfloat16 [4096, 4, 4096], P('mp', 'section')
- grad_bias: float32 [4, 4096], P('section', 'mp')
The draws below stay inside these ranges and needn't reach their ends.
All inputs are finite; a program needn't handle non-finite values.
Results may differ from the reference program's by a relative error of at most 0.009.
Values may be sent and summed in bfloat16 or wider, within the bound.
A program may use at most 64 MiB of HBM per device.

```python
import math
import jax
import jax.numpy as jnp
from jax import lax

D = 4096
LAYERS = 4
HID = 4096
TOKENS = 64


def draw_activations(key, part):
    keys = jax.random.split(jax.random.fold_in(key, 11), 2)
    position = jnp.arange(TOKENS, dtype=jnp.float32)
    ramp = 1.0 + 2.0 * position / max(TOKENS - 1, 1)
    jitter = jnp.exp(jax.random.uniform(keys[1], (LAYERS, TOKENS, 1), jnp.float32, -0.4, 0.4))
    scale_rows = ramp[None, :, None] * jitter
    base = jax.random.normal(keys[0], (LAYERS, TOKENS, D), jnp.float32)
    return jnp.clip(base * scale_rows, -24.0, 24.0).astype(jnp.bfloat16)


def draw_dec_weight(key, part):
    keys = jax.random.split(jax.random.fold_in(key, 23), 4)
    row_scale = jnp.exp(jax.random.uniform(keys[1], (HID, 1, 1), jnp.float32, math.log(0.3), math.log(3.0)))
    col_scale = jnp.exp(jax.random.uniform(keys[2], (1, 1, D), jnp.float32, math.log(0.3), math.log(3.0)))
    level = jnp.arange(LAYERS, dtype=jnp.float32)
    layer_ramp = 0.5 + level / max(LAYERS - 1, 1)
    layer_jitter = jnp.exp(jax.random.uniform(keys[3], (HID, LAYERS, 1), jnp.float32, -0.5, 0.5))
    layer_scale = layer_ramp[None, :, None] * layer_jitter
    base = jnp.clip(jax.random.normal(keys[0], (HID, LAYERS, D), jnp.float32), -6.0, 6.0)
    return (base * row_scale * col_scale * layer_scale / math.sqrt(HID)).astype(jnp.bfloat16)


def level_of(own_key, shape, pieces, smallest, high):
    gain, own = 1.0, jax.random.fold_in(own_key, 6)
    for axis_at, shards_of in pieces:
        steps = jnp.exp(jax.random.uniform(jax.random.fold_in(own, axis_at), (shards_of,), jnp.float32, smallest / len(pieces), high / len(pieces)))
        gain = gain * jnp.repeat(steps, shape[axis_at] // shards_of).reshape([-1 if axis == axis_at else 1 for axis in range(len(shape))])
    return gain


def centred(rng, shape, spread, limit, cuts=(), held_as=jnp.bfloat16):
    level = level_of(rng, shape, cuts, -0.22, 0.18) if cuts else 1.0
    drawn = jax.random.normal(rng, shape, jnp.float32) * spread * level
    return jnp.minimum(jnp.maximum(drawn, -limit), limit).astype(held_as)


def setup_inputs(seed: int = 0) -> dict:
    streams_of = jax.random.split(jax.random.key(seed), 6)
    activations = draw_activations(jax.random.fold_in(streams_of[5], 71), 0)
    enc_weight = centred(streams_of[1], (LAYERS, D, HID), (LAYERS * D) ** -0.5, 0.046875, ((0, 4), (2, 8)))
    enc_bias = centred(streams_of[2], (HID,), 1.0, 4.0, ((0, 8),), jnp.float32)
    dec_weight = draw_dec_weight(jax.random.fold_in(streams_of[5], 71), 0)
    dec_bias = centred(streams_of[4], (LAYERS, D), 0.5, 3.0, ((0, 4),), jnp.float32)
    return dict(activations=activations, enc_weight=enc_weight, enc_bias=enc_bias, dec_weight=dec_weight, dec_bias=dec_bias)


penalty_weight = 2.0

def reference(activations, enc_weight, enc_bias, dec_weight, dec_bias):
    token_count = activations.shape[1]
    pre_sum = jnp.zeros((token_count, enc_weight.shape[2]), jnp.float32) + enc_bias[None, :]
    for layer in range(LAYERS):
        pre_sum = pre_sum + jnp.dot(activations[layer], enc_weight[layer], preferred_element_type=jnp.float32)
    latents = jnp.maximum(pre_sum, 0.0).astype(jnp.bfloat16)
    latent_sum = lax.optimization_barrier(jnp.sum(latents.astype(jnp.float32), axis=0))
    norm_total = jnp.zeros((enc_weight.shape[2],), jnp.float32)
    square_sum = jnp.zeros((), jnp.float32)
    grad_list = []
    bias_list = []
    for layer in range(LAYERS):
        w_layer = dec_weight[:, layer, :]
        layer_norm = jnp.sqrt(lax.optimization_barrier(jnp.sum(jnp.square(w_layer.astype(jnp.float32)), axis=1)) + 1e-06)
        norm_total = norm_total + layer_norm
        recon = jnp.dot(latents, w_layer, preferred_element_type=jnp.float32) + dec_bias[layer][None, :]
        error = recon - activations[layer].astype(jnp.float32)
        square_sum = square_sum + jnp.sum(error * error)
        scaled = 2.0 * error / token_count
        grad_rec = scaled.astype(jnp.bfloat16)
        bias_list.append(lax.optimization_barrier(jnp.sum(scaled, axis=0)))
        grad_sum = jnp.dot(latents.T, grad_rec, preferred_element_type=jnp.float32)
        coef = penalty_weight * latent_sum / token_count / layer_norm
        grad_list.append((grad_sum + coef[:, None] * w_layer.astype(jnp.float32)).astype(jnp.bfloat16))
    penalty_part = penalty_weight / token_count * jnp.sum(latents.astype(jnp.float32) * norm_total[None, :])
    loss = square_sum / token_count + penalty_part
    grad_dec = jnp.stack(grad_list, axis=1)
    grad_bias = jnp.stack(bias_list, axis=0)
    return (loss, grad_dec, grad_bias)
```

```python
import functools

import jax
import jax.numpy as jnp
from jax import lax
from jax.experimental import pallas as pl
from jax.experimental.pallas import tpu as pltpu
from jax.sharding import PartitionSpec as P

penalty_weight = 2.0
PAIR = 2
F32 = jnp.float32
BF16 = jnp.bfloat16
MESH = pl.DeviceIdType.MESH


def pack(rows):
    half = rows.shape[-1] // 2
    return jnp.concatenate([rows[..., :half], rows[..., half:]], axis=-2).astype(BF16)


def loop(count, body):
    if count == 1:
        body(0)
    else:
        pl.loop(0, count)(body)


def comm_kernel(
    n, ns, C, HC,
    act, enc_hbm, bias, dec_hbm, dbias,
    loss_out, g_out, lat_out, coef_out,
    x_all, g_all, enc_v, dec_v, part, rs, rs1, rs2s, rs2r, norm, loss_s, loss_m,
    load_sem, xs_sem, xr_sem, gs_sem, gr_sem, ps_sem, pr_sem,
    r1s_sem, r1r_sem, r2s_sem, r2r_sem, ls_sem, lr_sem, ms_sem, mr_sem,
):
    A = n // PAIR
    T = n * 8
    TB = min(n, 8)
    sec = lax.axis_index("section")
    me = lax.axis_index("mp")
    a, b = me // PAIR, lax.rem(me, PAIR)
    ob = 1 - b
    partner = a * PAIR + ob
    half = x_all.shape[2]
    hid = enc_v.shape[1]

    barrier = pltpu.get_barrier_semaphore()
    for k in range(1, n):
        pl.semaphore_signal(barrier, inc=1, device_id={"mp": lax.rem(me + k, n)}, device_id_type=MESH)
    for k in range(1, ns):
        pl.semaphore_signal(barrier, inc=1, device_id={"section": lax.rem(sec + k, ns)}, device_id_type=MESH)

    enc_copy = pltpu.make_async_copy(enc_hbm, enc_v, load_sem.at[0])
    dec_copy = pltpu.make_async_copy(dec_hbm, dec_v, load_sem.at[1])
    enc_copy.start()
    dec_copy.start()

    x_all[me] = pack(act[...].astype(F32))
    pl.semaphore_wait(barrier, n - 1 + ns - 1)

    def remote(src, dst, ssem, rsem, axis, peer):
        return pltpu.make_async_remote_copy(
            src_ref=src, dst_ref=dst, send_sem=ssem, recv_sem=rsem,
            device_id={axis: peer}, device_id_type=MESH,
        )

    def gather_copy(buf, ssem, rsem, slot, index, peer):
        return remote(buf.at[slot], buf.at[slot], ssem.at[index], rsem.at[slot], "mp", peer)

    def gather_start(buf, ssem, rsem):
        copies = []
        for k in range(1, A):
            peer = lax.rem(a + k, A) * PAIR + b
            copies.append(gather_copy(buf, ssem, rsem, me, k - 1, peer))
        copies.append(gather_copy(buf, ssem, rsem, me, A - 1, partner))
        for c in copies[-1:] + copies[:-1]:
            c.start()
        return copies

    def gather_forward(buf, ssem, rsem):
        copies = []
        for k in range(1, A):
            slot = lax.rem(a + A - k, A) * PAIR + b
            c = gather_copy(buf, ssem, rsem, slot, A - 1 + k, partner)
            c.wait_recv()
            c.start()
            copies.append(c)
        return copies

    def gather_finish(buf, ssem, rsem, copies):
        for k in range(A):
            slot = lax.rem(a + A - k, A) * PAIR + ob
            gather_copy(buf, ssem, rsem, slot, 0, partner).wait_recv()
        for c in copies:
            c.wait_send()

    x_copies = gather_start(x_all, xs_sem, xr_sem)
    dec_copy.wait()

    @pl.loop(0, hid // 32)
    def _(i):
        rows = pl.ds(pl.multiple_of(i * 32, 32), 32)
        acc = jnp.zeros((32, 128), F32)
        for k in range(dec_v.shape[1] // 128):
            w = dec_v[rows, k * 128:(k + 1) * 128].astype(F32)
            acc = acc + w * w
        total = jnp.sum(acc, axis=1, keepdims=True)
        norm[rows, :] = jnp.broadcast_to(jnp.sqrt(total + 1e-06), (32, 128))

    x_copies += gather_forward(x_all, xs_sem, xr_sem)
    enc_copy.wait()
    gather_finish(x_all, xs_sem, xr_sem, x_copies)

    hw = hid // HC
    p_copies = []
    for h in range(HC):
        def enc_step(i, h=h):
            blocks = pl.ds(i * TB, TB)
            x = x_all[blocks].reshape(TB * 16, half)
            lo = jnp.dot(x, enc_v[:half, h * hw:(h + 1) * hw], preferred_element_type=F32)
            hi = jnp.dot(x, enc_v[half:, h * hw:(h + 1) * hw], preferred_element_type=F32)
            lo = lo.reshape(TB, 16, hw)[:, :8]
            hi = hi.reshape(TB, 16, hw)[:, 8:]
            rows = pl.ds(pl.multiple_of(i * TB * 8, TB * 8), TB * 8)
            part[h, sec, rows, :] = (lo + hi).reshape(TB * 8, hw).astype(BF16)

        loop(n // TB, enc_step)
        for k in range(1, ns):
            peer = lax.rem(sec + k, ns)
            c = remote(part.at[h, sec], part.at[h, sec], ps_sem.at[h, k - 1], pr_sem.at[h, sec], "section", peer)
            c.start()
            p_copies.append(c)
    for h in range(HC):
        for k in range(1, ns):
            src = lax.rem(sec + k, ns)
            remote(part.at[h, src], part.at[h, src], ps_sem.at[h, k - 1], pr_sem.at[h, src], "section", src).wait_recv()
        cols = slice(h * hw, (h + 1) * hw)

        def lat_step(i, h=h, cols=cols):
            rows = pl.ds(pl.multiple_of(i * TB * 8, TB * 8), TB * 8)
            pre = bias[:, cols]
            for s in range(ns):
                pre = pre + part[h, s, rows, :].astype(F32)
            lat_out[rows, cols] = jnp.maximum(pre, 0.0).astype(BF16)

        loop(n // TB, lat_step)

    cw = half // C

    def block(c, dest):
        return rs.at[c, dest]

    r1_copies = []
    for c in range(C):
        def dec_step(i, c=c):
            rows = pl.ds(pl.multiple_of(i * TB * 8, TB * 8), TB * 8)
            lat = lat_out[rows, :]
            lo = jnp.dot(lat, dec_v[:, c * cw:(c + 1) * cw], preferred_element_type=F32)
            hi = jnp.dot(lat, dec_v[:, half + c * cw:half + (c + 1) * cw], preferred_element_type=F32)
            both = jnp.concatenate([lo.reshape(TB, 8, cw), hi.reshape(TB, 8, cw)], axis=1)
            rs[c, pl.ds(i * TB, TB)] = both.astype(BF16)

        loop(n // TB, dec_step)
        for k in range(1, A + 1):
            row = lax.rem(a + k, A)
            cp = remote(rs.at[c, row * PAIR + ob], rs1.at[c, row], r1s_sem.at[c, k - 1], r1r_sem.at[c, row], "mp", partner)
            cp.start()
            r1_copies.append(cp)

    ones = jnp.ones((T, 128), BF16)
    lat_sum = lax.dot_general(lat_out[...], ones, (((0,), (0,)), ((), ())), preferred_element_type=F32)
    coef_out[...] = penalty_weight * lat_sum / T / norm[...]
    penalty = penalty_weight / T * jnp.sum(lat_sum[:, :1] * norm[:, :1])

    r2_copies = []
    for c in range(C):
        for k in range(1, A):
            row = lax.rem(a + k, A)
            remote(rs.at[c, 0], rs1.at[c, row], r1s_sem.at[c, k - 1], r1r_sem.at[c, row], "mp", partner).wait_recv()
            rs2s[c, row] = (rs[c, row * PAIR + b].astype(F32) + rs1[c, row].astype(F32)).astype(BF16)
            cp = remote(rs2s.at[c, row], rs2r.at[c, a], r2s_sem.at[c, k - 1], r2r_sem.at[c, a], "mp", row * PAIR + b)
            cp.start()
            r2_copies.append(cp)
    squares = jnp.zeros((), F32)
    for c in range(C):
        remote(rs.at[c, 0], rs1.at[c, a], r1s_sem.at[c, A - 1], r1r_sem.at[c, a], "mp", partner).wait_recv()
        total = rs[c, me].astype(F32) + rs1[c, a].astype(F32)
        for k in range(1, A):
            row = lax.rem(a + A - k, A)
            remote(rs2s.at[c, row], rs2r.at[c, row], r2s_sem.at[c, k - 1], r2r_sem.at[c, row], "mp", partner).wait_recv()
            total = total + rs2r[c, row].astype(F32)
        lo = slice(c * cw, (c + 1) * cw)
        hi = slice(half + c * cw, half + (c + 1) * cw)
        own = jnp.concatenate([act[:, lo].astype(F32), act[:, hi].astype(F32)], axis=0)
        shift = jnp.concatenate([jnp.broadcast_to(dbias[:, lo], (8, cw)), jnp.broadcast_to(dbias[:, hi], (8, cw))], axis=0)
        error = total + shift - own
        squares = squares + jnp.sum(error * error)
        g_all[me, :, lo] = (2.0 * error / T).astype(BF16)

    g_copies = gather_start(g_all, gs_sem, gr_sem)
    loss_s[sec] = jnp.full((8, 128), squares / T + penalty, F32)
    l_copies = []
    for k in range(1, ns):
        peer = lax.rem(sec + k, ns)
        cp = remote(loss_s.at[sec], loss_s.at[sec], ls_sem.at[k - 1], lr_sem.at[sec], "section", peer)
        cp.start()
        l_copies.append(cp)
    for cp in p_copies + r1_copies + r2_copies:
        cp.wait_send()
    for k in range(1, ns):
        src = lax.rem(sec + k, ns)
        remote(loss_s.at[src], loss_s.at[src], ls_sem.at[k - 1], lr_sem.at[src], "section", src).wait_recv()
    total = loss_s[0]
    for s in range(1, ns):
        total = total + loss_s[s]
    loss_m[me] = total
    for k in range(1, n):
        peer = lax.rem(me + k, n)
        cp = remote(loss_m.at[me], loss_m.at[me], ms_sem.at[k - 1], mr_sem.at[me], "mp", peer)
        cp.start()
        l_copies.append(cp)
    g_copies += gather_forward(g_all, gs_sem, gr_sem)
    for k in range(1, n):
        src = lax.rem(me + k, n)
        remote(loss_m.at[src], loss_m.at[src], ms_sem.at[k - 1], mr_sem.at[src], "mp", src).wait_recv()
    total = loss_m[0]
    for s in range(1, n):
        total = total + loss_m[s]
    loss_out[...] = total
    gather_finish(g_all, gs_sem, gr_sem, g_copies)

    def out_step(i):
        g_out[pl.ds(i * TB, TB)] = g_all[pl.ds(i * TB, TB)]

    loop(n // TB, out_step)
    for cp in l_copies:
        cp.wait_send()


def grad_kernel(blocks, g, lat, coef, w, out, bias_out, spread):
    step = pl.program_id(0)
    n = g.shape[0]
    per = pl.num_programs(0) // 2

    @pl.when(step == 0)
    def _():
        rows = lat[...].astype(F32).reshape(n, 8, lat.shape[1])
        zero = jnp.zeros_like(rows)
        spread[0] = jnp.concatenate([rows, zero], axis=1).astype(BF16).reshape(n * 16, lat.shape[1])
        spread[1] = jnp.concatenate([zero, rows], axis=1).astype(BF16).reshape(n * 16, lat.shape[1])

    side = step // per
    cw = out.shape[1]
    cols = pl.ds(pl.multiple_of(lax.rem(step, per) * cw, cw), cw)
    gb = g[:, :, cols]
    sides = jnp.sum(gb.astype(F32), axis=0)
    lo = jnp.sum(sides[:8], axis=0, keepdims=True)
    hi = jnp.sum(sides[8:], axis=0, keepdims=True)
    bias_out[...] = jnp.where(side == 0, lo, hi)
    total = lax.dot_general(
        spread[side], gb.reshape(n * 16, cw), (((0,), (0,)), ((), ())), preferred_element_type=F32
    )
    out[...] = (total + coef[:, :1] * w[...].astype(F32)).astype(BF16)


def local(ns, n, activations, enc_weight, enc_bias, dec_weight, dec_bias):
    act = activations[0]
    enc = enc_weight[0]
    w_dec = dec_weight[:, 0, :]
    rows, d = act.shape
    hid = enc.shape[1]
    T = rows * n
    half = d // 2
    A = n // PAIR
    C, HC = 2, 2
    vmem = pl.BlockSpec(memory_space=pltpu.VMEM)
    anys = pl.BlockSpec(memory_space=pl.ANY)
    dma = pltpu.SemaphoreType.DMA
    loss, g, lat, coef = pl.pallas_call(
        functools.partial(comm_kernel, n, ns, C, HC),
        out_shape=(
            jax.ShapeDtypeStruct((8, 128), F32),
            jax.ShapeDtypeStruct((n, 16, half), BF16),
            jax.ShapeDtypeStruct((T, hid), BF16),
            jax.ShapeDtypeStruct((hid, 128), F32),
        ),
        in_specs=[vmem, anys, vmem, anys, vmem],
        out_specs=[vmem] * 4,
        scratch_shapes=[
            pltpu.VMEM((n, 16, half), BF16),
            pltpu.VMEM((n, 16, half), BF16),
            pltpu.VMEM((d, hid), BF16),
            pltpu.VMEM((hid, d), BF16),
            pltpu.VMEM((HC, ns, T, hid // HC), BF16),
            pltpu.VMEM((C, n, 16, half // C), BF16),
            pltpu.VMEM((C, A, 16, half // C), BF16),
            pltpu.VMEM((C, A, 16, half // C), BF16),
            pltpu.VMEM((C, A, 16, half // C), BF16),
            pltpu.VMEM((hid, 128), F32),
            pltpu.VMEM((ns, 8, 128), F32),
            pltpu.VMEM((n, 8, 128), F32),
            dma((2,)),
            dma((2 * A,)), dma((n,)),
            dma((2 * A,)), dma((n,)),
            dma((HC, ns)), dma((HC, ns)),
            dma((C, A)), dma((C, A)),
            dma((C, A)), dma((C, A)),
            dma((ns,)), dma((ns,)),
            dma((n,)), dma((n,)),
        ],
        compiler_params=pltpu.CompilerParams(
            collective_id=0, has_side_effects=True, vmem_limit_bytes=48 * 1024 * 1024
        ),
        name="crosscoder_comm",
    )(act, enc, enc_bias[None, :], w_dec, dec_bias)

    steps = 8
    cw = d // steps
    grad_dec, bias_sum = pl.pallas_call(
        functools.partial(grad_kernel, steps),
        grid=(steps,),
        out_shape=(
            jax.ShapeDtypeStruct((hid, d), BF16),
            jax.ShapeDtypeStruct((1, d), F32),
        ),
        in_specs=[vmem, vmem, vmem, pl.BlockSpec((hid, cw), lambda i: (0, i))],
        out_specs=[pl.BlockSpec((hid, cw), lambda i: (0, i)), pl.BlockSpec((1, cw), lambda i: (0, i))],
        scratch_shapes=[pltpu.VMEM((2, n * 16, hid), BF16)],
        name="grad_dec",
    )(g, lat, coef, w_dec)
    width = d // n
    grad_bias = lax.dynamic_slice_in_dim(bias_sum, lax.axis_index("mp") * width, width, 1)
    return loss[0, 0], grad_dec[:, None, :], grad_bias


def solution(mesh):
    in_specs = (
        P("section", "mp", None),
        P("section", None, "mp"),
        P("mp"),
        P("mp", "section", None),
        P("section", None),
    )
    out_specs = (P(), P("mp", "section", None), P("section", "mp"))
    body = functools.partial(local, mesh.shape["section"], mesh.shape["mp"])
    return jax.shard_map(body, mesh=mesh, in_specs=in_specs, out_specs=out_specs, check_vma=False)
```

```python
import functools

import jax
import jax.numpy as jnp
from jax import lax
from jax.experimental import pallas as pl
from jax.experimental.pallas import tpu as pltpu
from jax.sharding import PartitionSpec as P

penalty_weight = 2.0
PAIR = 2
STEPS = 8
F32 = jnp.float32
BF16 = jnp.bfloat16
MESH = pl.DeviceIdType.MESH


def pack(rows):
    half = rows.shape[-1] // 2
    return jnp.concatenate([rows[..., :half], rows[..., half:]], axis=-2).astype(BF16)


def loop(count, body):
    if count == 1:
        body(0)
    else:
        pl.loop(0, count)(body)


def comm_kernel(
    n, ns, C, HC,
    act_hbm, enc_hbm, bias_hbm, dec_hbm, dbias_hbm,
    loss_out, g_out, spread_out, coef_out,
    act, bias, dbias, lat_out, x_all, g_all, enc_v, dec_v, part, rs, rs1, rs2s, rs2r, norm, loss_s, loss_m,
    load_sem, xs_sem, xr_sem, gs_sem, gr_sem, ps_sem, pr_sem,
    r1s_sem, r1r_sem, r2s_sem, r2r_sem, ls_sem, lr_sem, ms_sem, mr_sem,
):
    A = n // PAIR
    T = n * 8
    TB = min(n, 8)
    sec = lax.axis_index("section")
    me = lax.axis_index("mp")
    a, b = me // PAIR, lax.rem(me, PAIR)
    ob = 1 - b
    partner = a * PAIR + ob
    half = x_all.shape[2]
    hid = enc_v.shape[1]

    barrier = pltpu.get_barrier_semaphore()
    for k in range(1, n):
        pl.semaphore_signal(barrier, inc=1, device_id={"mp": lax.rem(me + k, n)}, device_id_type=MESH)
    for k in range(1, ns):
        pl.semaphore_signal(barrier, inc=1, device_id={"section": lax.rem(sec + k, ns)}, device_id_type=MESH)

    act_copy = pltpu.make_async_copy(act_hbm, act, load_sem.at[0])
    enc_copy = pltpu.make_async_copy(enc_hbm, enc_v, load_sem.at[1])
    dec_copy = pltpu.make_async_copy(dec_hbm, dec_v, load_sem.at[2])
    bias_copy = pltpu.make_async_copy(bias_hbm, bias, load_sem.at[3])
    dbias_copy = pltpu.make_async_copy(dbias_hbm, dbias, load_sem.at[4])
    for c in (act_copy, dec_copy, enc_copy, bias_copy, dbias_copy):
        c.start()
    act_copy.wait()

    x_all[me] = pack(act[...].astype(F32))
    pl.semaphore_wait(barrier, n - 1 + ns - 1)

    def remote(src, dst, ssem, rsem, axis, peer):
        return pltpu.make_async_remote_copy(
            src_ref=src, dst_ref=dst, send_sem=ssem, recv_sem=rsem,
            device_id={axis: peer}, device_id_type=MESH,
        )

    def gather_copy(buf, ssem, rsem, slot, index, peer):
        return remote(buf.at[slot], buf.at[slot], ssem.at[index], rsem.at[slot], "mp", peer)

    def gather_start(buf, ssem, rsem):
        copies = []
        for k in range(1, A):
            peer = lax.rem(a + k, A) * PAIR + b
            copies.append(gather_copy(buf, ssem, rsem, me, k - 1, peer))
        copies.append(gather_copy(buf, ssem, rsem, me, A - 1, partner))
        for c in copies[-1:] + copies[:-1]:
            c.start()
        return copies

    def gather_forward(buf, ssem, rsem):
        copies = []
        for k in range(1, A):
            slot = lax.rem(a + A - k, A) * PAIR + b
            c = gather_copy(buf, ssem, rsem, slot, A - 1 + k, partner)
            c.wait_recv()
            c.start()
            copies.append(c)
        return copies

    def gather_finish(buf, ssem, rsem, copies):
        for k in range(A):
            slot = lax.rem(a + A - k, A) * PAIR + ob
            gather_copy(buf, ssem, rsem, slot, 0, partner).wait_recv()
        for c in copies:
            c.wait_send()

    x_copies = gather_start(x_all, xs_sem, xr_sem)
    dec_copy.wait()

    @pl.loop(0, hid // 32)
    def _(i):
        rows = pl.ds(pl.multiple_of(i * 32, 32), 32)
        acc = jnp.zeros((32, 128), F32)
        for k in range(dec_v.shape[1] // 128):
            w = dec_v[rows, k * 128:(k + 1) * 128].astype(F32)
            acc = acc + w * w
        total = jnp.sum(acc, axis=1, keepdims=True)
        norm[rows, :] = jnp.broadcast_to(jnp.sqrt(total + 1e-06), (32, 128))

    x_copies += gather_forward(x_all, xs_sem, xr_sem)
    for c in (enc_copy, bias_copy, dbias_copy):
        c.wait()
    gather_finish(x_all, xs_sem, xr_sem, x_copies)

    hw = hid // HC
    p_copies = []
    for h in range(HC):
        def enc_step(i, h=h):
            blocks = pl.ds(i * TB, TB)
            x = x_all[blocks].reshape(TB * 16, half)
            lo = jnp.dot(x, enc_v[:half, h * hw:(h + 1) * hw], preferred_element_type=F32)
            hi = jnp.dot(x, enc_v[half:, h * hw:(h + 1) * hw], preferred_element_type=F32)
            lo = lo.reshape(TB, 16, hw)[:, :8]
            hi = hi.reshape(TB, 16, hw)[:, 8:]
            rows = pl.ds(pl.multiple_of(i * TB * 8, TB * 8), TB * 8)
            part[h, sec, rows, :] = (lo + hi).reshape(TB * 8, hw).astype(BF16)

        loop(n // TB, enc_step)
        for k in range(1, ns):
            peer = lax.rem(sec + k, ns)
            c = remote(part.at[h, sec], part.at[h, sec], ps_sem.at[h, k - 1], pr_sem.at[h, sec], "section", peer)
            c.start()
            p_copies.append(c)
    for h in range(HC):
        for k in range(1, ns):
            src = lax.rem(sec + k, ns)
            remote(part.at[h, src], part.at[h, src], ps_sem.at[h, k - 1], pr_sem.at[h, src], "section", src).wait_recv()
        cols = slice(h * hw, (h + 1) * hw)

        def lat_step(i, h=h, cols=cols):
            rows = pl.ds(pl.multiple_of(i * TB * 8, TB * 8), TB * 8)
            pre = bias[:, cols]
            for s in range(ns):
                pre = pre + part[h, s, rows, :].astype(F32)
            lat_out[rows, cols] = jnp.maximum(pre, 0.0).astype(BF16)

        loop(n // TB, lat_step)

    cw = half // C

    def block(c, dest):
        return rs.at[c, dest]

    r1_copies = []
    for c in range(C):
        def dec_step(i, c=c):
            rows = pl.ds(pl.multiple_of(i * TB * 8, TB * 8), TB * 8)
            lat = lat_out[rows, :]
            lo = jnp.dot(lat, dec_v[:, c * cw:(c + 1) * cw], preferred_element_type=F32)
            hi = jnp.dot(lat, dec_v[:, half + c * cw:half + (c + 1) * cw], preferred_element_type=F32)
            both = jnp.concatenate([lo.reshape(TB, 8, cw), hi.reshape(TB, 8, cw)], axis=1)
            rs[c, pl.ds(i * TB, TB)] = both.astype(BF16)

        loop(n // TB, dec_step)
        for k in range(1, A + 1):
            row = lax.rem(a + k, A)
            cp = remote(rs.at[c, row * PAIR + ob], rs1.at[c, row], r1s_sem.at[c, k - 1], r1r_sem.at[c, row], "mp", partner)
            cp.start()
            r1_copies.append(cp)

    ones = jnp.ones((T, 128), BF16)
    lat_sum = lax.dot_general(lat_out[...], ones, (((0,), (0,)), ((), ())), preferred_element_type=F32)
    coef_out[...] = penalty_weight * lat_sum / T / norm[...]
    penalty = penalty_weight / T * jnp.sum(lat_sum[:, :1] * norm[:, :1])

    r2_copies = []
    for c in range(C):
        for k in range(1, A):
            row = lax.rem(a + k, A)
            remote(rs.at[c, 0], rs1.at[c, row], r1s_sem.at[c, k - 1], r1r_sem.at[c, row], "mp", partner).wait_recv()
            rs2s[c, row] = (rs[c, row * PAIR + b].astype(F32) + rs1[c, row].astype(F32)).astype(BF16)
            cp = remote(rs2s.at[c, row], rs2r.at[c, a], r2s_sem.at[c, k - 1], r2r_sem.at[c, a], "mp", row * PAIR + b)
            cp.start()
            r2_copies.append(cp)
    squares = jnp.zeros((), F32)
    for c in range(C):
        remote(rs.at[c, 0], rs1.at[c, a], r1s_sem.at[c, A - 1], r1r_sem.at[c, a], "mp", partner).wait_recv()
        total = rs[c, me].astype(F32) + rs1[c, a].astype(F32)
        for k in range(1, A):
            row = lax.rem(a + A - k, A)
            remote(rs2s.at[c, row], rs2r.at[c, row], r2s_sem.at[c, k - 1], r2r_sem.at[c, row], "mp", partner).wait_recv()
            total = total + rs2r[c, row].astype(F32)
        lo = slice(c * cw, (c + 1) * cw)
        hi = slice(half + c * cw, half + (c + 1) * cw)
        own = jnp.concatenate([act[:, lo].astype(F32), act[:, hi].astype(F32)], axis=0)
        shift = jnp.concatenate([jnp.broadcast_to(dbias[:, lo], (8, cw)), jnp.broadcast_to(dbias[:, hi], (8, cw))], axis=0)
        error = total + shift - own
        squares = squares + jnp.sum(error * error)
        g_all[me, :, lo] = (2.0 * error / T).astype(BF16)

    g_copies = gather_start(g_all, gs_sem, gr_sem)
    loss_s[sec] = jnp.full((8, 128), squares / T + penalty, F32)
    l_copies = []
    for k in range(1, ns):
        peer = lax.rem(sec + k, ns)
        cp = remote(loss_s.at[sec], loss_s.at[sec], ls_sem.at[k - 1], lr_sem.at[sec], "section", peer)
        cp.start()
        l_copies.append(cp)
    for cp in p_copies + r1_copies + r2_copies:
        cp.wait_send()
    for k in range(1, ns):
        src = lax.rem(sec + k, ns)
        remote(loss_s.at[src], loss_s.at[src], ls_sem.at[k - 1], lr_sem.at[src], "section", src).wait_recv()
    total = loss_s[0]
    for s in range(1, ns):
        total = total + loss_s[s]
    loss_m[me] = total
    for k in range(1, n):
        peer = lax.rem(me + k, n)
        cp = remote(loss_m.at[me], loss_m.at[me], ms_sem.at[k - 1], mr_sem.at[me], "mp", peer)
        cp.start()
        l_copies.append(cp)
    g_copies += gather_forward(g_all, gs_sem, gr_sem)
    wide = lat_out[...].astype(F32).reshape(n, 8, hid)
    zero = jnp.zeros_like(wide)
    spread_out[0] = jnp.concatenate([wide, zero], axis=1).reshape(n * 16, hid).T.astype(BF16)
    spread_out[1] = jnp.concatenate([zero, wide], axis=1).reshape(n * 16, hid).T.astype(BF16)

    for k in range(1, n):
        src = lax.rem(me + k, n)
        remote(loss_m.at[src], loss_m.at[src], ms_sem.at[k - 1], mr_sem.at[src], "mp", src).wait_recv()
    total = loss_m[0]
    for s in range(1, n):
        total = total + loss_m[s]
    loss_out[...] = total
    gather_finish(g_all, gs_sem, gr_sem, g_copies)

    def out_step(i):
        g_out[pl.ds(i * TB, TB)] = g_all[pl.ds(i * TB, TB)]

    loop(n // TB, out_step)
    for cp in l_copies:
        cp.wait_send()


def grad_kernel(loss, g, spread, coef, w, loss_out, out, bias_out):
    step = pl.program_id(0)
    n = g.shape[0]
    per = pl.num_programs(0) // 2
    hid, cw = out.shape

    @pl.when(step == 0)
    def _():
        loss_out[...] = loss[:1, :1]

    side = step // per
    cols = pl.ds(pl.multiple_of(lax.rem(step, per) * cw, cw), cw)
    gb = g[:, :, cols]

    def bias_step():
        sums = jnp.sum(gb.astype(F32), axis=0)
        lo = jnp.sum(sums[:8], axis=0, keepdims=True)
        hi = jnp.sum(sums[8:], axis=0, keepdims=True)
        bias_out[...] = jnp.where(side == 0, lo, hi)

    if bias_out.shape[1] == cw and STEPS == n:
        pl.when(step == lax.axis_index("mp"))(bias_step)
    else:
        bias_step()
    gm = gb.reshape(n * 16, cw)
    wcols = pl.ds(pl.multiple_of(step * cw, cw), cw)
    for r in range(0, hid, 128):
        total = jnp.dot(spread[side, r:r + 128, :], gm, preferred_element_type=F32)
        scale = jnp.concatenate([coef[r:r + 128, :]] * (cw // 128), axis=1)
        out[r:r + 128, :] = (total + scale * w[r:r + 128, wcols].astype(F32)).astype(BF16)


def local(ns, n, activations, enc_weight, enc_bias, dec_weight, dec_bias):
    act = activations[0]
    enc = enc_weight[0]
    w_dec = dec_weight[:, 0, :]
    rows, d = act.shape
    hid = enc.shape[1]
    T = rows * n
    half = d // 2
    A = n // PAIR
    C, HC = 2, 2
    vmem = pl.BlockSpec(memory_space=pltpu.VMEM)
    hbm = pl.BlockSpec(memory_space=pltpu.HBM)
    dma = pltpu.SemaphoreType.DMA
    loss, g, spread, coef = pl.pallas_call(
        functools.partial(comm_kernel, n, ns, C, HC),
        out_shape=(
            jax.ShapeDtypeStruct((8, 128), F32),
            jax.ShapeDtypeStruct((n, 16, half), BF16),
            jax.ShapeDtypeStruct((2, hid, n * 16), BF16),
            jax.ShapeDtypeStruct((hid, 128), F32),
        ),
        in_specs=[hbm] * 5,
        out_specs=[vmem] * 4,
        scratch_shapes=[
            pltpu.VMEM((rows, d), BF16),
            pltpu.VMEM((1, hid), F32),
            pltpu.VMEM((1, d), F32),
            pltpu.VMEM((T, hid), BF16),
            pltpu.VMEM((n, 16, half), BF16),
            pltpu.VMEM((n, 16, half), BF16),
            pltpu.VMEM((d, hid), BF16),
            pltpu.VMEM((hid, d), BF16),
            pltpu.VMEM((HC, ns, T, hid // HC), BF16),
            pltpu.VMEM((C, n, 16, half // C), BF16),
            pltpu.VMEM((C, A, 16, half // C), BF16),
            pltpu.VMEM((C, A, 16, half // C), BF16),
            pltpu.VMEM((C, A, 16, half // C), BF16),
            pltpu.VMEM((hid, 128), F32),
            pltpu.VMEM((ns, 8, 128), F32),
            pltpu.VMEM((n, 8, 128), F32),
            dma((5,)),
            dma((2 * A,)), dma((n,)),
            dma((2 * A,)), dma((n,)),
            dma((HC, ns)), dma((HC, ns)),
            dma((C, A)), dma((C, A)),
            dma((C, A)), dma((C, A)),
            dma((ns,)), dma((ns,)),
            dma((n,)), dma((n,)),
        ],
        compiler_params=pltpu.CompilerParams(
            collective_id=0, has_side_effects=True, vmem_limit_bytes=(28 + n // 4) * 1024 * 1024
        ),
        name="crosscoder_comm",
    )(*(pltpu.with_memory_space_constraint(v, pltpu.HBM) for v in (act, enc, enc_bias[None, :], w_dec, dec_bias)))

    steps = STEPS
    cw, width = d // steps, d // n
    own = steps == n
    loss, grad_dec, bias = pl.pallas_call(
        grad_kernel,
        grid=(steps,),
        out_shape=(
            jax.ShapeDtypeStruct((1, 1), F32),
            jax.ShapeDtypeStruct((hid, d), BF16),
            jax.ShapeDtypeStruct((1, width if own else d), F32),
        ),
        in_specs=[vmem] * 5,
        out_specs=[
            pl.BlockSpec((1, 1), lambda i: (0, 0)),
            pl.BlockSpec((hid, cw), lambda i: (0, i)),
            pl.BlockSpec((1, cw), lambda i: (0, 0) if own else (0, i)),
        ],
        compiler_params=pltpu.CompilerParams(vmem_limit_bytes=18 * 1024 * 1024),
        name="grad_dec",
    )(loss, g, spread, coef, w_dec)
    if not own:
        bias = lax.dynamic_slice_in_dim(bias, lax.axis_index("mp") * width, width, 1)
    return loss.reshape(()), grad_dec[:, None, :], bias


def solution(mesh):
    in_specs = (
        P("section", "mp", None),
        P("section", None, "mp"),
        P("mp"),
        P("mp", "section", None),
        P("section", None),
    )
    out_specs = (P(), P("mp", "section", None), P("section", "mp"))
    body = functools.partial(local, mesh.shape["section"], mesh.shape["mp"])
    return jax.shard_map(body, mesh=mesh, in_specs=in_specs, out_specs=out_specs, check_vma=False)
```

```python
import functools

import jax
import jax.numpy as jnp
from jax import lax
from jax.experimental import pallas as pl
from jax.experimental.pallas import tpu as pltpu
from jax.sharding import PartitionSpec as P

penalty_weight = 2.0
PAIR = 2
F32 = jnp.float32
BF16 = jnp.bfloat16
MESH = pl.DeviceIdType.MESH


def loop(count, body):
    if count == 1:
        body(0)
    else:
        pl.loop(0, count)(body)


def comm_kernel(
    n, ns, C, HC,
    act_hbm, enc_hbm, bias_hbm, dec_hbm, dbias_hbm,
    loss_out, g_out, spread_out, coef_out, first_out, sums_out,
    act, bias, dbias, lat_out, x_all, g_all, enc_v, dec_v, acc_v, part, rs, rs1, rs2s, rs2r, norm, loss_s, loss_m,
    load_sem, xs_sem, xr_sem, gs_sem, gr_sem, ps_sem, pr_sem,
    r1s_sem, r1r_sem, r2s_sem, r2r_sem, ls_sem, lr_sem, ms_sem, mr_sem,
):
    A = n // PAIR
    T = n * 8
    TB = min(n, 8)
    sec = lax.axis_index("section")
    me = lax.axis_index("mp")
    a, b = me // PAIR, lax.rem(me, PAIR)
    ob = 1 - b
    partner = a * PAIR + ob
    half = dec_v.shape[1] // 2
    cw = half // C
    hid = enc_v.shape[1]

    barrier = pltpu.get_barrier_semaphore()
    for k in range(1, n):
        pl.semaphore_signal(barrier, inc=1, device_id={"mp": lax.rem(me + k, n)}, device_id_type=MESH)
    for k in range(1, ns):
        pl.semaphore_signal(barrier, inc=1, device_id={"section": lax.rem(sec + k, ns)}, device_id_type=MESH)

    act_copy = pltpu.make_async_copy(act_hbm, act, load_sem.at[0])
    enc_copy = pltpu.make_async_copy(enc_hbm, enc_v, load_sem.at[1])
    dec_copy = pltpu.make_async_copy(dec_hbm, dec_v, load_sem.at[2])
    bias_copy = pltpu.make_async_copy(bias_hbm, bias, load_sem.at[3])
    dbias_copy = pltpu.make_async_copy(dbias_hbm, dbias, load_sem.at[4])
    for c in (act_copy, dec_copy, enc_copy, bias_copy, dbias_copy):
        c.start()
    act_copy.wait()

    def cols_of(c):
        return slice(c * cw, (c + 1) * cw), slice(half + c * cw, half + (c + 1) * cw)

    for c in range(C):
        lo, hi = cols_of(c)
        x_all[c, me] = jnp.concatenate([act[:, lo].astype(F32), act[:, hi].astype(F32)], axis=0).astype(BF16)
    pl.semaphore_wait(barrier, n - 1 + ns - 1)

    def remote(src, dst, ssem, rsem, axis, peer):
        return pltpu.make_async_remote_copy(
            src_ref=src, dst_ref=dst, send_sem=ssem, recv_sem=rsem,
            device_id={axis: peer}, device_id_type=MESH,
        )

    def gather_copy(buf, ssem, rsem, c, slot, index, peer):
        return remote(buf.at[c, slot], buf.at[c, slot], ssem.at[c, index], rsem.at[c, slot], "mp", peer)

    def gather_start(buf, ssem, rsem, c):
        copies = [gather_copy(buf, ssem, rsem, c, me, A - 1, partner)]
        for k in range(1, A):
            peer = lax.rem(a + k, A) * PAIR + b
            copies.append(gather_copy(buf, ssem, rsem, c, me, k - 1, peer))
        for cp in copies:
            cp.start()
        return copies

    def gather_forward(buf, ssem, rsem, c):
        copies = []
        for k in range(1, A):
            slot = lax.rem(a + A - k, A) * PAIR + b
            cp = gather_copy(buf, ssem, rsem, c, slot, A - 1 + k, partner)
            cp.wait_recv()
            cp.start()
            copies.append(cp)
        return copies

    def gather_finish(buf, ssem, rsem, c):
        for k in range(A):
            slot = lax.rem(a + A - k, A) * PAIR + ob
            gather_copy(buf, ssem, rsem, c, slot, 0, partner).wait_recv()

    x_copies = []
    for c in range(C):
        x_copies += gather_start(x_all, xs_sem, xr_sem, c)
    dec_copy.wait()

    @pl.loop(0, hid // 32)
    def _(i):
        rows = pl.ds(pl.multiple_of(i * 32, 32), 32)
        acc = jnp.zeros((32, 128), F32)
        for k in range(dec_v.shape[1] // 128):
            w = dec_v[rows, k * 128:(k + 1) * 128].astype(F32)
            acc = acc + w * w
        total = jnp.sum(acc, axis=1, keepdims=True)
        norm[rows, :] = jnp.broadcast_to(jnp.sqrt(total + 1e-06), (32, 128))

    for c in range(C):
        x_copies += gather_forward(x_all, xs_sem, xr_sem, c)
    for cp in (enc_copy, bias_copy, dbias_copy):
        cp.wait()

    def enc_chunk(c, i, cols):
        lo, hi = cols_of(c)
        x = x_all[c, pl.ds(i * TB, TB)].reshape(TB * 16, cw)
        left = jnp.dot(x, enc_v[lo, cols], preferred_element_type=F32)
        right = jnp.dot(x, enc_v[hi, cols], preferred_element_type=F32)
        left = left.reshape(TB, 16, left.shape[1])[:, :8]
        right = right.reshape(TB, 16, right.shape[1])[:, 8:]
        return (left + right).reshape(TB * 8, left.shape[2])

    def rows_of(i):
        return pl.ds(pl.multiple_of(i * TB * 8, TB * 8), TB * 8)

    for c in range(C - 1):
        gather_finish(x_all, xs_sem, xr_sem, c)

        def early(i, c=c):
            value = enc_chunk(c, i, slice(0, hid))
            acc_v[rows_of(i), :] = value if c == 0 else acc_v[rows_of(i), :] + value

        loop(n // TB, early)
    gather_finish(x_all, xs_sem, xr_sem, C - 1)

    hw = hid // HC
    p_copies = []
    for h in range(HC):
        def enc_step(i, h=h):
            cols = slice(h * hw, (h + 1) * hw)
            value = acc_v[rows_of(i), cols] + enc_chunk(C - 1, i, cols)
            part[h, sec, rows_of(i), :] = value.astype(BF16)

        loop(n // TB, enc_step)
        for k in range(1, ns):
            peer = lax.rem(sec + k, ns)
            c = remote(part.at[h, sec], part.at[h, sec], ps_sem.at[h, k - 1], pr_sem.at[h, sec], "section", peer)
            c.start()
            p_copies.append(c)
    for h in range(HC):
        for k in range(1, ns):
            src = lax.rem(sec + k, ns)
            remote(part.at[h, src], part.at[h, src], ps_sem.at[h, k - 1], pr_sem.at[h, src], "section", src).wait_recv()
        cols = slice(h * hw, (h + 1) * hw)

        def lat_step(i, h=h, cols=cols):
            rows = pl.ds(pl.multiple_of(i * TB * 8, TB * 8), TB * 8)
            pre = bias[:, cols]
            for s in range(ns):
                pre = pre + part[h, s, rows, :].astype(F32)
            lat_out[rows, cols] = jnp.maximum(pre, 0.0).astype(BF16)

        loop(n // TB, lat_step)

    def r1_start(c, k):
        row = lax.rem(a + k, A)
        cp = remote(rs.at[c, row * PAIR + ob], rs1.at[c, row], r1s_sem.at[c, k - 1], r1r_sem.at[c, row], "mp", partner)
        cp.start()
        return cp

    r1_copies = []
    for c in range(C):
        def dec_step(i, c=c):
            rows = pl.ds(pl.multiple_of(i * TB * 8, TB * 8), TB * 8)
            lat = lat_out[rows, :]
            lo = jnp.dot(lat, dec_v[:, c * cw:(c + 1) * cw], preferred_element_type=F32)
            hi = jnp.dot(lat, dec_v[:, half + c * cw:half + (c + 1) * cw], preferred_element_type=F32)
            both = jnp.concatenate([lo.reshape(TB, 8, cw), hi.reshape(TB, 8, cw)], axis=1)
            rs[c, pl.ds(i * TB, TB)] = both.astype(BF16)

        loop(n // TB, dec_step)
        for k in range(1, A):
            r1_copies.append(r1_start(c, k))
    for c in range(C):
        r1_copies.append(r1_start(c, A))

    ones = jnp.ones((T, 128), BF16)
    lat_sum = lax.dot_general(lat_out[...], ones, (((0,), (0,)), ((), ())), preferred_element_type=F32)
    coef_out[...] = penalty_weight * lat_sum / T / norm[...]
    penalty = penalty_weight / T * jnp.sum(lat_sum[:, :1] * norm[:, :1])

    r2_copies = []
    for c in range(C):
        for k in range(1, A):
            row = lax.rem(a + k, A)
            remote(rs.at[c, 0], rs1.at[c, row], r1s_sem.at[c, k - 1], r1r_sem.at[c, row], "mp", partner).wait_recv()
            rs2s[c, row] = (rs[c, row * PAIR + b].astype(F32) + rs1[c, row].astype(F32)).astype(BF16)
            cp = remote(rs2s.at[c, row], rs2r.at[c, a], r2s_sem.at[c, k - 1], r2r_sem.at[c, a], "mp", row * PAIR + b)
            cp.start()
            r2_copies.append(cp)
    wide = lat_out[...].astype(F32).reshape(n, 8, hid)
    zero = jnp.zeros_like(wide)
    spread_out[0] = jnp.concatenate([wide, zero], axis=1).reshape(n * 16, hid).T.astype(BF16)
    spread_out[1] = jnp.concatenate([zero, wide], axis=1).reshape(n * 16, hid).T.astype(BF16)

    squares = jnp.zeros((), F32)
    g_copies = []
    for c in range(C):
        remote(rs.at[c, 0], rs1.at[c, a], r1s_sem.at[c, A - 1], r1r_sem.at[c, a], "mp", partner).wait_recv()
        total = rs[c, me].astype(F32) + rs1[c, a].astype(F32)
        for k in range(1, A):
            row = lax.rem(a + A - k, A)
            remote(rs2s.at[c, row], rs2r.at[c, row], r2s_sem.at[c, k - 1], r2r_sem.at[c, row], "mp", partner).wait_recv()
            total = total + rs2r[c, row].astype(F32)
        lo, hi = cols_of(c)
        own = jnp.concatenate([act[:, lo].astype(F32), act[:, hi].astype(F32)], axis=0)
        shift = jnp.concatenate([jnp.broadcast_to(dbias[:, lo], (8, cw)), jnp.broadcast_to(dbias[:, hi], (8, cw))], axis=0)
        error = total + shift - own
        squares = squares + jnp.sum(error * error)
        g_all[c, me] = (2.0 * error / T).astype(BF16)
        g_copies += gather_start(g_all, gs_sem, gr_sem, c)

    loss_s[sec] = jnp.full((8, 128), squares / T + penalty, F32)
    l_copies = []
    for k in range(1, ns):
        peer = lax.rem(sec + k, ns)
        cp = remote(loss_s.at[sec], loss_s.at[sec], ls_sem.at[k - 1], lr_sem.at[sec], "section", peer)
        cp.start()
        l_copies.append(cp)
    for c in range(C - 1):
        g_copies += gather_forward(g_all, gs_sem, gr_sem, c)
    for cp in x_copies + p_copies + r1_copies + r2_copies:
        cp.wait_send()
    for k in range(1, ns):
        src = lax.rem(sec + k, ns)
        remote(loss_s.at[src], loss_s.at[src], ls_sem.at[k - 1], lr_sem.at[src], "section", src).wait_recv()
    total = loss_s[0]
    for s in range(1, ns):
        total = total + loss_s[s]
    loss_m[me] = total
    for k in range(1, n):
        peer = lax.rem(me + k, n)
        cp = remote(loss_m.at[me], loss_m.at[me], ms_sem.at[k - 1], mr_sem.at[me], "mp", peer)
        cp.start()
        l_copies.append(cp)
    g_copies += gather_forward(g_all, gs_sem, gr_sem, C - 1)
    for c in range(C - 1):
        gather_finish(g_all, gs_sem, gr_sem, c)
        sums_out[2 * c], sums_out[2 * c + 1] = column_sums(g_all[c])
        for side in range(2):
            cols = cols_of(c)[side]
            for r in range(0, cw, 512):
                grad_block(
                    first_out.at[2 * c + side, :, r:r + 512], spread_out.at[side],
                    g_all[c, :, :, r:r + 512].reshape(n * 16, 512), coef_out,
                    dec_v.at[:, cols.start + r:cols.start + r + 512],
                )
    for k in range(1, n):
        src = lax.rem(me + k, n)
        remote(loss_m.at[src], loss_m.at[src], ms_sem.at[k - 1], mr_sem.at[src], "mp", src).wait_recv()
    total = loss_m[0]
    for s in range(1, n):
        total = total + loss_m[s]
    loss_out[...] = total
    gather_finish(g_all, gs_sem, gr_sem, C - 1)

    def out_step(i):
        g_out[pl.ds(i * TB, TB)] = g_all[C - 1, pl.ds(i * TB, TB)]

    loop(n // TB, out_step)
    for cp in l_copies + g_copies:
        cp.wait_send()


def column_sums(g):
    sums = jnp.sum(g.astype(F32), axis=0)
    shape = (8, sums.shape[1])
    return tuple(
        jnp.broadcast_to(jnp.sum(sums[r:r + 8], axis=0, keepdims=True), shape) for r in (0, 8)
    )


def grad_block(out, spread, g, coef, w):
    width = out.shape[1]
    for r in range(0, out.shape[0], 128):
        total = jnp.dot(spread[r:r + 128, :], g, preferred_element_type=F32)
        scale = jnp.concatenate([coef[r:r + 128, :]] * (width // 128), axis=1)
        out[r:r + 128, :] = (total + scale * w[r:r + 128, :].astype(F32)).astype(BF16)


def grad_kernel(C, width, loss, g, spread, coef, first, sums, w, loss_out, out, bias_out, rest, all_sums, sem):
    n, cw = g.shape[0], g.shape[2]
    half = w.shape[1] // 2
    copies = []
    for c in range(C - 1):
        for side in range(2):
            i = 2 * c + side
            cols = slice(side * half + c * cw, side * half + (c + 1) * cw)
            cp = pltpu.make_async_copy(first.at[i], out.at[:, cols], sem.at[i])
            cp.start()
            copies.append(cp)
    for i in range(2 * (C - 1)):
        all_sums[i] = sums[i]
    slot = 2 * (C - 1)
    for side in range(2):
        for r in range(0, cw, 512):
            start = side * half + (C - 1) * cw + r
            piece = rest.at[side, :, r:r + 512]
            grad_block(piece, spread.at[side], g[:, :, r:r + 512].reshape(n * 16, 512), coef, w.at[:, start:start + 512])
            cp = pltpu.make_async_copy(piece, out.at[:, start:start + 512], sem.at[slot])
            cp.start()
            copies.append(cp)
            slot += 1
    all_sums[2 * C - 2], all_sums[2 * C - 1] = column_sums(g[...])
    loss_out[...] = loss[:1, :1]
    if width % 128 == 0 and cw % width == 0:
        me = lax.axis_index("mp")
        side, place = me // (n // 2), lax.rem(me, n // 2)
        per = cw // width
        cols = pl.ds(pl.multiple_of(lax.rem(place, per) * width, width), width)
        bias_out[...] = all_sums[2 * (place // per) + side, 0:1, cols]
    else:
        for c in range(C):
            for side in range(2):
                start = side * half + c * cw
                bias_out[:, start:start + cw] = all_sums[2 * c + side, 0:1, :]
    for cp in copies:
        cp.wait()


def local(ns, n, activations, enc_weight, enc_bias, dec_weight, dec_bias):
    act = activations[0]
    enc = enc_weight[0]
    w_dec = dec_weight[:, 0, :]
    rows, d = act.shape
    hid = enc.shape[1]
    T = rows * n
    half = d // 2
    A = n // PAIR
    C, HC = 2, 2
    vmem = pl.BlockSpec(memory_space=pltpu.VMEM)
    hbm = pl.BlockSpec(memory_space=pltpu.HBM)
    dma = pltpu.SemaphoreType.DMA
    cw = half // C
    loss, g, spread, coef, first, sums = pl.pallas_call(
        functools.partial(comm_kernel, n, ns, C, HC),
        out_shape=(
            jax.ShapeDtypeStruct((8, 128), F32),
            jax.ShapeDtypeStruct((n, 16, cw), BF16),
            jax.ShapeDtypeStruct((2, hid, n * 16), BF16),
            jax.ShapeDtypeStruct((hid, 128), F32),
            jax.ShapeDtypeStruct((2 * (C - 1), hid, cw), BF16),
            jax.ShapeDtypeStruct((2 * (C - 1), 8, cw), F32),
        ),
        in_specs=[hbm] * 5,
        out_specs=[vmem] * 6,
        scratch_shapes=[
            pltpu.VMEM((rows, d), BF16),
            pltpu.VMEM((1, hid), F32),
            pltpu.VMEM((1, d), F32),
            pltpu.VMEM((T, hid), BF16),
            pltpu.VMEM((C, n, 16, cw), BF16),
            pltpu.VMEM((C, n, 16, cw), BF16),
            pltpu.VMEM((d, hid), BF16),
            pltpu.VMEM((hid, d), BF16),
            pltpu.VMEM((T, hid), F32),
            pltpu.VMEM((HC, ns, T, hid // HC), BF16),
            pltpu.VMEM((C, n, 16, half // C), BF16),
            pltpu.VMEM((C, A, 16, half // C), BF16),
            pltpu.VMEM((C, A, 16, half // C), BF16),
            pltpu.VMEM((C, A, 16, half // C), BF16),
            pltpu.VMEM((hid, 128), F32),
            pltpu.VMEM((ns, 8, 128), F32),
            pltpu.VMEM((n, 8, 128), F32),
            dma((5,)),
            dma((C, 2 * A)), dma((C, n)),
            dma((C, 2 * A)), dma((C, n)),
            dma((HC, ns)), dma((HC, ns)),
            dma((C, A)), dma((C, A)),
            dma((C, A)), dma((C, A)),
            dma((ns,)), dma((ns,)),
            dma((n,)), dma((n,)),
        ],
        compiler_params=pltpu.CompilerParams(
            collective_id=0, has_side_effects=True, vmem_limit_bytes=(28 + n // 4) * 1024 * 1024
        ),
        name="crosscoder_comm",
    )(*(pltpu.with_memory_space_constraint(v, pltpu.HBM) for v in (act, enc, enc_bias[None, :], w_dec, dec_bias)))

    width = d // n
    own = width % 128 == 0 and cw % width == 0
    loss, grad_dec, bias = pl.pallas_call(
        functools.partial(grad_kernel, C, width),
        out_shape=(
            jax.ShapeDtypeStruct((1, 1), F32),
            jax.ShapeDtypeStruct((hid, d), BF16),
            jax.ShapeDtypeStruct((1, width if own else d), F32),
        ),
        in_specs=[vmem] * 7,
        out_specs=[vmem, hbm, vmem],
        scratch_shapes=[
            pltpu.VMEM((2, hid, cw), BF16),
            pltpu.VMEM((2 * C, 8, cw), F32),
            dma((2 * (C - 1) + 2 * (cw // 512),)),
        ],
        compiler_params=pltpu.CompilerParams(vmem_limit_bytes=18 * 1024 * 1024),
        name="grad_dec",
    )(loss, g, spread, coef, first, sums, w_dec)
    if not own:
        bias = lax.dynamic_slice_in_dim(bias, lax.axis_index("mp") * width, width, 1)
    return loss.reshape(()), grad_dec[:, None, :], bias


def solution(mesh):
    in_specs = (
        P("section", "mp", None),
        P("section", None, "mp"),
        P("mp"),
        P("mp", "section", None),
        P("section", None),
    )
    out_specs = (P(), P("mp", "section", None), P("section", "mp"))
    body = functools.partial(local, mesh.shape["section"], mesh.shape["mp"])
    return jax.shard_map(body, mesh=mesh, in_specs=in_specs, out_specs=out_specs, check_vma=False)
```

```python
import functools

import jax
import jax.numpy as jnp
from jax import lax
from jax.experimental import pallas as pl
from jax.experimental.pallas import tpu as pltpu
from jax.sharding import PartitionSpec as P

penalty_weight = 2.0
PAIR = 2
F32 = jnp.float32
BF16 = jnp.bfloat16
MESH = pl.DeviceIdType.MESH


def loop(count, body):
    if count == 1:
        body(0)
    else:
        pl.loop(0, count)(body)


def comm_kernel(
    n, ns, CX, C, CR, HC,
    act_hbm, enc_hbm, bias_hbm, dec_hbm, dbias_hbm,
    loss_out, g_out, spread_out, coef_out, first_out, sums_out,
    act, bias, dbias, lat_out, x_all, g_all, enc_v, dec_v, acc_v, part, rs, rs1, rs2s, rs2r, norm, loss_s, loss_m,
    load_sem, xs_sem, xr_sem, gs_sem, gr_sem, ps_sem, pr_sem,
    r1s_sem, r1r_sem, r2s_sem, r2r_sem, ls_sem, lr_sem, ms_sem, mr_sem,
):
    A = n // PAIR
    T = n * 8
    TB = min(n, 8)
    sec = lax.axis_index("section")
    me = lax.axis_index("mp")
    a, b = me // PAIR, lax.rem(me, PAIR)
    ob = 1 - b
    partner = a * PAIR + ob
    half = dec_v.shape[1] // 2
    cw = half // C
    hid = enc_v.shape[1]

    barrier = pltpu.get_barrier_semaphore()
    for k in range(1, n):
        pl.semaphore_signal(barrier, inc=1, device_id={"mp": lax.rem(me + k, n)}, device_id_type=MESH)
    for k in range(1, ns):
        pl.semaphore_signal(barrier, inc=1, device_id={"section": lax.rem(sec + k, ns)}, device_id_type=MESH)

    act_copy = pltpu.make_async_copy(act_hbm, act, load_sem.at[0])
    enc_copy = pltpu.make_async_copy(enc_hbm, enc_v, load_sem.at[1])
    dec_copy = pltpu.make_async_copy(dec_hbm, dec_v, load_sem.at[2])
    bias_copy = pltpu.make_async_copy(bias_hbm, bias, load_sem.at[3])
    dbias_copy = pltpu.make_async_copy(dbias_hbm, dbias, load_sem.at[4])
    for c in (act_copy, dec_copy, enc_copy, bias_copy, dbias_copy):
        c.start()
    act_copy.wait()

    def cols_of(c):
        return slice(c * cw, (c + 1) * cw), slice(half + c * cw, half + (c + 1) * cw)

    xw = half // CX

    def cols_x(c):
        return slice(c * xw, (c + 1) * xw), slice(half + c * xw, half + (c + 1) * xw)

    for c in range(CX):
        lo, hi = cols_x(c)
        x_all[c, me] = jnp.concatenate([act[:, lo].astype(F32), act[:, hi].astype(F32)], axis=0).astype(BF16)
    pl.semaphore_wait(barrier, n - 1 + ns - 1)

    def remote(src, dst, ssem, rsem, axis, peer):
        return pltpu.make_async_remote_copy(
            src_ref=src, dst_ref=dst, send_sem=ssem, recv_sem=rsem,
            device_id={axis: peer}, device_id_type=MESH,
        )

    def gather_copy(buf, ssem, rsem, c, slot, index, peer):
        return remote(buf.at[c, slot], buf.at[c, slot], ssem.at[c, index], rsem.at[c, slot], "mp", peer)

    def gather_start(buf, ssem, rsem, c):
        copies = [gather_copy(buf, ssem, rsem, c, me, A - 1, partner)]
        for k in range(1, A):
            peer = lax.rem(a + k, A) * PAIR + b
            copies.append(gather_copy(buf, ssem, rsem, c, me, k - 1, peer))
        for cp in copies:
            cp.start()
        return copies

    def gather_forward(buf, ssem, rsem, c):
        copies = []
        for k in range(1, A):
            slot = lax.rem(a + A - k, A) * PAIR + b
            cp = gather_copy(buf, ssem, rsem, c, slot, A - 1 + k, partner)
            cp.wait_recv()
            cp.start()
            copies.append(cp)
        return copies

    def gather_finish(buf, ssem, rsem, c):
        for k in range(A):
            slot = lax.rem(a + A - k, A) * PAIR + ob
            gather_copy(buf, ssem, rsem, c, slot, 0, partner).wait_recv()

    x_copies = []
    for c in range(CX):
        x_copies += gather_start(x_all, xs_sem, xr_sem, c)
    dec_copy.wait()

    @pl.loop(0, hid // 32)
    def _(i):
        rows = pl.ds(pl.multiple_of(i * 32, 32), 32)
        acc = jnp.zeros((32, 128), F32)
        for k in range(dec_v.shape[1] // 128):
            w = dec_v[rows, k * 128:(k + 1) * 128].astype(F32)
            acc = acc + w * w
        total = jnp.sum(acc, axis=1, keepdims=True)
        norm[rows, :] = jnp.broadcast_to(jnp.sqrt(total + 1e-06), (32, 128))

    x_copies += gather_forward(x_all, xs_sem, xr_sem, 0)
    for cp in (enc_copy, bias_copy, dbias_copy):
        cp.wait()

    def enc_chunk(c, i, cols):
        lo, hi = cols_x(c)
        x = x_all[c, pl.ds(i * TB, TB)].reshape(TB * 16, xw)
        left = jnp.dot(x, enc_v[lo, cols], preferred_element_type=F32)
        right = jnp.dot(x, enc_v[hi, cols], preferred_element_type=F32)
        left = left.reshape(TB, 16, left.shape[1])[:, :8]
        right = right.reshape(TB, 16, right.shape[1])[:, 8:]
        return (left + right).reshape(TB * 8, left.shape[2])

    def rows_of(i):
        return pl.ds(pl.multiple_of(i * TB * 8, TB * 8), TB * 8)

    for c in range(CX - 1):
        x_copies += gather_forward(x_all, xs_sem, xr_sem, c + 1)
        gather_finish(x_all, xs_sem, xr_sem, c)

        def early(i, c=c):
            value = enc_chunk(c, i, slice(0, hid))
            acc_v[rows_of(i), :] = value if c == 0 else acc_v[rows_of(i), :] + value

        loop(n // TB, early)
    gather_finish(x_all, xs_sem, xr_sem, CX - 1)

    hw = hid // HC
    p_copies = []
    for h in range(HC):
        def enc_step(i, h=h):
            cols = slice(h * hw, (h + 1) * hw)
            value = enc_chunk(CX - 1, i, cols)
            if CX > 1:
                value = acc_v[rows_of(i), cols] + value
            part[h, sec, rows_of(i), :] = value.astype(BF16)

        loop(n // TB, enc_step)
        for k in range(1, ns):
            peer = lax.rem(sec + k, ns)
            c = remote(part.at[h, sec], part.at[h, sec], ps_sem.at[h, k - 1], pr_sem.at[h, sec], "section", peer)
            c.start()
            p_copies.append(c)
    for h in range(HC):
        for k in range(1, ns):
            src = lax.rem(sec + k, ns)
            remote(part.at[h, src], part.at[h, src], ps_sem.at[h, k - 1], pr_sem.at[h, src], "section", src).wait_recv()
        cols = slice(h * hw, (h + 1) * hw)

        def lat_step(i, h=h, cols=cols):
            rows = pl.ds(pl.multiple_of(i * TB * 8, TB * 8), TB * 8)
            pre = bias[:, cols]
            for s in range(ns):
                pre = pre + part[h, s, rows, :].astype(F32)
            lat_out[rows, cols] = jnp.maximum(pre, 0.0).astype(BF16)

        loop(n // TB, lat_step)

    rw = half // CR

    def r1_start(c, k):
        row = lax.rem(a + k, A)
        cp = remote(rs.at[c, row * PAIR + ob], rs1.at[c, row], r1s_sem.at[c, k - 1], r1r_sem.at[c, row], "mp", partner)
        cp.start()
        return cp

    r1_copies = []
    for c in range(CR):
        def dec_step(i, c=c):
            rows = pl.ds(pl.multiple_of(i * TB * 8, TB * 8), TB * 8)
            lat = lat_out[rows, :]
            lo = jnp.dot(lat, dec_v[:, c * rw:(c + 1) * rw], preferred_element_type=F32)
            hi = jnp.dot(lat, dec_v[:, half + c * rw:half + (c + 1) * rw], preferred_element_type=F32)
            both = jnp.concatenate([lo.reshape(TB, 8, rw), hi.reshape(TB, 8, rw)], axis=1)
            rs[c, pl.ds(i * TB, TB)] = both.astype(BF16)

        loop(n // TB, dec_step)
        for k in range(1, A):
            r1_copies.append(r1_start(c, k))
    for c in range(CR):
        r1_copies.append(r1_start(c, A))

    ones = jnp.ones((T, 128), BF16)
    lat_sum = lax.dot_general(lat_out[...], ones, (((0,), (0,)), ((), ())), preferred_element_type=F32)
    coef_out[...] = penalty_weight * lat_sum / T / norm[...]
    penalty = penalty_weight / T * jnp.sum(lat_sum[:, :1] * norm[:, :1])

    r2_copies = []
    for c in range(CR):
        for k in range(1, A):
            row = lax.rem(a + k, A)
            remote(rs.at[c, 0], rs1.at[c, row], r1s_sem.at[c, k - 1], r1r_sem.at[c, row], "mp", partner).wait_recv()
            rs2s[c, row] = (rs[c, row * PAIR + b].astype(F32) + rs1[c, row].astype(F32)).astype(BF16)
            cp = remote(rs2s.at[c, row], rs2r.at[c, a], r2s_sem.at[c, k - 1], r2r_sem.at[c, a], "mp", row * PAIR + b)
            cp.start()
            r2_copies.append(cp)
    wide = lat_out[...].astype(F32).reshape(n, 8, hid)
    zero = jnp.zeros_like(wide)
    spread_out[0] = jnp.concatenate([wide, zero], axis=1).reshape(n * 16, hid).T.astype(BF16)
    spread_out[1] = jnp.concatenate([zero, wide], axis=1).reshape(n * 16, hid).T.astype(BF16)

    squares = jnp.zeros((), F32)
    g_copies = []
    per = CR // C
    for c in range(CR):
        remote(rs.at[c, 0], rs1.at[c, a], r1s_sem.at[c, A - 1], r1r_sem.at[c, a], "mp", partner).wait_recv()
        total = rs[c, me].astype(F32) + rs1[c, a].astype(F32)
        for k in range(1, A):
            row = lax.rem(a + A - k, A)
            remote(rs2s.at[c, row], rs2r.at[c, row], r2s_sem.at[c, k - 1], r2r_sem.at[c, row], "mp", partner).wait_recv()
            total = total + rs2r[c, row].astype(F32)
        lo, hi = slice(c * rw, (c + 1) * rw), slice(half + c * rw, half + (c + 1) * rw)
        own = jnp.concatenate([act[:, lo].astype(F32), act[:, hi].astype(F32)], axis=0)
        shift = jnp.concatenate([jnp.broadcast_to(dbias[:, lo], (8, rw)), jnp.broadcast_to(dbias[:, hi], (8, rw))], axis=0)
        error = total + shift - own
        squares = squares + jnp.sum(error * error)
        place = c % per * rw
        g_all[c // per, me, :, place:place + rw] = (2.0 * error / T).astype(BF16)
        if c % per == per - 1:
            g_copies += gather_start(g_all, gs_sem, gr_sem, c // per)

    loss_s[sec] = jnp.full((8, 128), squares / T + penalty, F32)
    l_copies = []
    for k in range(1, ns):
        peer = lax.rem(sec + k, ns)
        cp = remote(loss_s.at[sec], loss_s.at[sec], ls_sem.at[k - 1], lr_sem.at[sec], "section", peer)
        cp.start()
        l_copies.append(cp)
    g_copies += gather_forward(g_all, gs_sem, gr_sem, 0)
    for cp in x_copies + p_copies + r1_copies + r2_copies:
        cp.wait_send()
    for k in range(1, ns):
        src = lax.rem(sec + k, ns)
        remote(loss_s.at[src], loss_s.at[src], ls_sem.at[k - 1], lr_sem.at[src], "section", src).wait_recv()
    total = loss_s[0]
    for s in range(1, ns):
        total = total + loss_s[s]
    loss_m[me] = total
    for k in range(1, n):
        peer = lax.rem(me + k, n)
        cp = remote(loss_m.at[me], loss_m.at[me], ms_sem.at[k - 1], mr_sem.at[me], "mp", peer)
        cp.start()
        l_copies.append(cp)
    for c in range(C - 1):
        g_copies += gather_forward(g_all, gs_sem, gr_sem, c + 1)
        gather_finish(g_all, gs_sem, gr_sem, c)
        sums_out[2 * c], sums_out[2 * c + 1] = column_sums(g_all[c])
        for side in range(2):
            cols = cols_of(c)[side]
            for r in range(0, cw, 512):
                grad_block(
                    first_out.at[2 * c + side, :, r:r + 512], spread_out.at[side],
                    g_all[c, :, :, r:r + 512].reshape(n * 16, 512), coef_out,
                    dec_v.at[:, cols.start + r:cols.start + r + 512],
                )
    for k in range(1, n):
        src = lax.rem(me + k, n)
        remote(loss_m.at[src], loss_m.at[src], ms_sem.at[k - 1], mr_sem.at[src], "mp", src).wait_recv()
    total = loss_m[0]
    for s in range(1, n):
        total = total + loss_m[s]
    loss_out[...] = total
    gather_finish(g_all, gs_sem, gr_sem, C - 1)

    def out_step(i):
        g_out[pl.ds(i * TB, TB)] = g_all[C - 1, pl.ds(i * TB, TB)]

    loop(n // TB, out_step)
    for cp in l_copies + g_copies:
        cp.wait_send()


def column_sums(g):
    sums = jnp.sum(g.astype(F32), axis=0)
    shape = (8, sums.shape[1])
    return tuple(
        jnp.broadcast_to(jnp.sum(sums[r:r + 8], axis=0, keepdims=True), shape) for r in (0, 8)
    )


def grad_block(out, spread, g, coef, w):
    width = out.shape[1]
    for r in range(0, out.shape[0], 128):
        total = jnp.dot(spread[r:r + 128, :], g, preferred_element_type=F32)
        scale = jnp.concatenate([coef[r:r + 128, :]] * (width // 128), axis=1)
        out[r:r + 128, :] = (total + scale * w[r:r + 128, :].astype(F32)).astype(BF16)


def grad_kernel(C, width, loss, g, spread, coef, first, sums, w, loss_out, out, bias_out, rest, all_sums, sem):
    n, cw = g.shape[0], g.shape[2]
    half = w.shape[1] // 2
    copies = []
    for c in range(C - 1):
        for side in range(2):
            i = 2 * c + side
            cols = slice(side * half + c * cw, side * half + (c + 1) * cw)
            cp = pltpu.make_async_copy(first.at[i], out.at[:, cols], sem.at[i])
            cp.start()
            copies.append(cp)
    for i in range(2 * (C - 1)):
        all_sums[i] = sums[i]
    slot = 2 * (C - 1)
    for side in range(2):
        for r in range(0, cw, 512):
            start = side * half + (C - 1) * cw + r
            piece = rest.at[side, :, r:r + 512]
            grad_block(piece, spread.at[side], g[:, :, r:r + 512].reshape(n * 16, 512), coef, w.at[:, start:start + 512])
            cp = pltpu.make_async_copy(piece, out.at[:, start:start + 512], sem.at[slot])
            cp.start()
            copies.append(cp)
            slot += 1
    all_sums[2 * C - 2], all_sums[2 * C - 1] = column_sums(g[...])
    loss_out[...] = loss[:1, :1]
    if width % 128 == 0 and cw % width == 0:
        me = lax.axis_index("mp")
        side, place = me // (n // 2), lax.rem(me, n // 2)
        per = cw // width
        cols = pl.ds(pl.multiple_of(lax.rem(place, per) * width, width), width)
        bias_out[...] = all_sums[2 * (place // per) + side, 0:1, cols]
    else:
        for c in range(C):
            for side in range(2):
                start = side * half + c * cw
                bias_out[:, start:start + cw] = all_sums[2 * c + side, 0:1, :]
    for cp in copies:
        cp.wait()


def local(ns, n, activations, enc_weight, enc_bias, dec_weight, dec_bias):
    act = activations[0]
    enc = enc_weight[0]
    w_dec = dec_weight[:, 0, :]
    rows, d = act.shape
    hid = enc.shape[1]
    T = rows * n
    half = d // 2
    A = n // PAIR
    CX, C, CR, HC = 1, 2, 4, 2
    vmem = pl.BlockSpec(memory_space=pltpu.VMEM)
    hbm = pl.BlockSpec(memory_space=pltpu.HBM)
    dma = pltpu.SemaphoreType.DMA
    cw = half // C
    loss, g, spread, coef, first, sums = pl.pallas_call(
        functools.partial(comm_kernel, n, ns, CX, C, CR, HC),
        out_shape=(
            jax.ShapeDtypeStruct((8, 128), F32),
            jax.ShapeDtypeStruct((n, 16, cw), BF16),
            jax.ShapeDtypeStruct((2, hid, n * 16), BF16),
            jax.ShapeDtypeStruct((hid, 128), F32),
            jax.ShapeDtypeStruct((2 * (C - 1), hid, cw), BF16),
            jax.ShapeDtypeStruct((2 * (C - 1), 8, cw), F32),
        ),
        in_specs=[hbm] * 5,
        out_specs=[vmem] * 6,
        scratch_shapes=[
            pltpu.VMEM((rows, d), BF16),
            pltpu.VMEM((1, hid), F32),
            pltpu.VMEM((1, d), F32),
            pltpu.VMEM((T, hid), BF16),
            pltpu.VMEM((CX, n, 16, half // CX), BF16),
            pltpu.VMEM((C, n, 16, cw), BF16),
            pltpu.VMEM((d, hid), BF16),
            pltpu.VMEM((hid, d), BF16),
            pltpu.VMEM((T, hid), F32),
            pltpu.VMEM((HC, ns, T, hid // HC), BF16),
            pltpu.VMEM((CR, n, 16, half // CR), BF16),
            pltpu.VMEM((CR, A, 16, half // CR), BF16),
            pltpu.VMEM((CR, A, 16, half // CR), BF16),
            pltpu.VMEM((CR, A, 16, half // CR), BF16),
            pltpu.VMEM((hid, 128), F32),
            pltpu.VMEM((ns, 8, 128), F32),
            pltpu.VMEM((n, 8, 128), F32),
            dma((5,)),
            dma((CX, 2 * A)), dma((CX, n)),
            dma((C, 2 * A)), dma((C, n)),
            dma((HC, ns)), dma((HC, ns)),
            dma((CR, A)), dma((CR, A)),
            dma((CR, A)), dma((CR, A)),
            dma((ns,)), dma((ns,)),
            dma((n,)), dma((n,)),
        ],
        compiler_params=pltpu.CompilerParams(
            collective_id=0, has_side_effects=True, vmem_limit_bytes=(28 + n // 4) * 1024 * 1024
        ),
        name="crosscoder_comm",
    )(*(pltpu.with_memory_space_constraint(v, pltpu.HBM) for v in (act, enc, enc_bias[None, :], w_dec, dec_bias)))

    width = d // n
    own = width % 128 == 0 and cw % width == 0
    loss, grad_dec, bias = pl.pallas_call(
        functools.partial(grad_kernel, C, width),
        out_shape=(
            jax.ShapeDtypeStruct((1, 1), F32),
            jax.ShapeDtypeStruct((hid, d), BF16),
            jax.ShapeDtypeStruct((1, width if own else d), F32),
        ),
        in_specs=[vmem] * 7,
        out_specs=[vmem, hbm, vmem],
        scratch_shapes=[
            pltpu.VMEM((2, hid, cw), BF16),
            pltpu.VMEM((2 * C, 8, cw), F32),
            dma((2 * (C - 1) + 2 * (cw // 512),)),
        ],
        compiler_params=pltpu.CompilerParams(vmem_limit_bytes=18 * 1024 * 1024),
        name="grad_dec",
    )(loss, g, spread, coef, first, sums, w_dec)
    if not own:
        bias = lax.dynamic_slice_in_dim(bias, lax.axis_index("mp") * width, width, 1)
    return loss.reshape(()), grad_dec[:, None, :], bias


def solution(mesh):
    in_specs = (
        P("section", "mp", None),
        P("section", None, "mp"),
        P("mp"),
        P("mp", "section", None),
        P("section", None),
    )
    out_specs = (P(), P("mp", "section", None), P("section", "mp"))
    body = functools.partial(local, mesh.shape["section"], mesh.shape["mp"])
    return jax.shard_map(body, mesh=mesh, in_specs=in_specs, out_specs=out_specs, check_vma=False)
```
